32 devices in a mesh: row: 4 (over z), col: 8 (over y, x, core).
Axes of the slice: x: 2, y: 2, z: 4, core: 2. Of those that a mesh axis runs over, the one named last changes fastest.
Arguments:
- a_trail: float32 [16384, 16384], P('row', 'col'), may hold values from -60 to 60, as said below
- a_panel: float32 [16384, 256], P(('row', 'col')), may hold values from -6 to 6
- l_panel: float32 [16384, 256], P(('row', 'col')), may hold values from -0.5 to 0.5
- a_diag: float32 [256, 256], replicated, may hold values from -60 to 60, as said below
- l_inverse: float32 [256, 256], replicated, may hold values from -4 to 4, as said below
Outputs:
- trail_out: float32 [16384, 16384], P('row', 'col')
- panel_out: float32 [16384, 256], P(('row', 'col'))
The draws below stay inside these ranges and needn't reach their ends.
Inputs may be any that keep to these rules, and one draw needn't show every extreme that they name: `a_trail`: symmetric. `a_diag`: symmetric. `l_inverse`: lower triangular with a positive diagonal.
All inputs are finite; a program needn't handle non-finite values.
Results may differ from the reference program's by a relative error of at most 0.0003.
Values sent between devices are 32-bit elements; how exact they have to be, the bound alone decides.
A program may use at most 192 MiB of HBM per device.

```python
import jax
import jax.numpy as jnp
from jax import lax

M = 16384
NB = 256
NS_STEPS = 8


def draw_a_trail(key, part):
    base = jax.random.normal(jax.random.fold_in(key, 11), (M, M), jnp.float32)
    sym = (base + base.T) * 0.7071067811865476
    return jnp.clip(sym, -60.0, 60.0)


def draw_a_diag(key, part):
    base = jax.random.normal(jax.random.fold_in(key, 21), (NB, NB), jnp.float32)
    sym = (base + base.T) * 0.7071067811865476
    return jnp.clip(sym, -60.0, 60.0)


def draw_l_inverse(key, part):
    lower = jnp.tril(jnp.ones((NB, NB), jnp.float32), -1)
    spread = 0.5 * jnp.clip(jax.random.normal(jax.random.fold_in(key, 31), (NB, NB), jnp.float32), -6.0, 6.0)
    diag_vals = jax.random.uniform(jax.random.fold_in(key, 32), (NB,), jnp.float32, 0.8, 1.2)
    off_part = spread * lower / jnp.sqrt(jnp.float32(NB))
    return off_part + jnp.diag(diag_vals)


def block_levels(rng, extent, split, least, high):
    level = 1.0
    for axis_at, shards_of in split:
        heights = jax.random.uniform(jax.random.fold_in(jax.random.fold_in(rng, 6), axis_at), (shards_of,), jnp.float32, least / len(split), high / len(split))
        level = level * jnp.repeat(jnp.exp(heights), extent[axis_at] // shards_of).reshape((-1,) + (1,) * (len(extent) - 1 - axis_at))
    return level


def gaussian(rng, extent, width, most, pieces=(), kind=jnp.bfloat16):
    factor_of = block_levels(rng, extent, pieces, -0.22, 0.18) if pieces else 1.0
    result = jax.random.normal(rng, extent, jnp.float32) * width * factor_of
    return jnp.minimum(jnp.maximum(result, -most), most).astype(kind)


def setup_inputs(seed: int = 0) -> dict:
    splits = jax.random.split(jax.random.key(seed), 6)
    a_trail = draw_a_trail(jax.random.fold_in(splits[5], 71), 0)
    a_panel = gaussian(splits[1], (M, NB), 1.0, 6.0, ((0, 32),), jnp.float32)
    l_panel = gaussian(splits[2], (M, NB), 0.0625, 0.5, ((0, 32),), jnp.float32)
    a_diag = draw_a_diag(jax.random.fold_in(splits[5], 71), 0)
    l_inverse = draw_l_inverse(jax.random.fold_in(splits[5], 71), 0)
    return dict(a_trail=a_trail, a_panel=a_panel, l_panel=l_panel, a_diag=a_diag, l_inverse=l_inverse)


def product(left, right):
    return jnp.dot(left.astype(jnp.float32), right.astype(jnp.float32), precision=lax.Precision.HIGHEST, preferred_element_type=jnp.float32)

def newton_inverse(matrix):
    identity = jnp.eye(matrix.shape[0], dtype=jnp.float32)
    approx = identity
    for repeat in range(NS_STEPS):
        approx = product(approx, 2.0 * identity - product(matrix, approx))
    return approx

def right_solve(factor, values):
    return lax.linalg.triangular_solve(factor, values, left_side=False, lower=True, transpose_a=True)

def reference(a_trail, a_panel, l_panel, a_diag, l_inverse):
    a11_new = product(product(l_inverse, a_diag), l_inverse.T)
    solved = product(a_panel, l_inverse.T)
    half_term = 0.5 * product(l_panel, a11_new)
    first_y = solved - half_term
    panel_out = first_y - half_term
    updated = a_trail - (product(first_y, l_panel.T) + product(l_panel, first_y.T))
    all_rows = jnp.arange(M, dtype=jnp.int32)
    keep_mask = (all_rows >= NB)[:, None]
    next_panel = jnp.where(keep_mask, updated[:, :NB], 0.0)
    picker = (all_rows[:, None] - NB == jnp.arange(NB, dtype=jnp.int32)[None, :]).astype(jnp.float32)
    gram = product(next_panel.T, next_panel)
    top_block = next_panel[NB:2 * NB]
    factor = jnp.linalg.cholesky(gram)
    q_rows = right_solve(factor, next_panel)
    q_top = right_solve(factor, top_block)
    identity = jnp.eye(NB, dtype=jnp.float32)
    g_inverse = newton_inverse(identity + q_top).T
    y_full = q_rows + picker
    x_mat = product(product(updated, y_full), g_inverse)
    m_core = product(g_inverse.T, product(y_full.T, x_mat))
    z_mat = x_mat - 0.5 * product(y_full, m_core)
    trail_out = updated - (product(z_mat, y_full.T) + product(y_full, z_mat.T))
    return (trail_out, panel_out)
```

```python
import functools

import jax
import jax.numpy as jnp
from jax import lax
from jax.experimental import pallas as pl
from jax.experimental.pallas import tpu as pltpu
from jax.sharding import PartitionSpec as P

NS_STEPS = 8
BOTH = ("row", "col")


def product(left, right):
    return jnp.dot(left, right, precision=lax.Precision.HIGHEST, preferred_element_type=jnp.float32)


def large_product(left, right):
    return jnp.dot(left, right, precision=lax.Precision.HIGH, preferred_element_type=jnp.float32)


def newton_inverse(matrix):
    identity = jnp.eye(matrix.shape[0], dtype=jnp.float32)
    approx = identity
    for repeat in range(NS_STEPS):
        approx = product(approx, 2.0 * identity - product(matrix, approx))
    return approx


def right_solve(factor, values):
    return lax.linalg.triangular_solve(
        factor, values, left_side=False, lower=True, transpose_a=True
    )


def sum_kernel(rows, cols, x_ref, o_ref, recv, red, send_a, recv_a, send_b, recv_b):
    count = rows * cols
    me = lax.axis_index("row") * cols + lax.axis_index("col")

    def peer(step):
        at = lax.rem(me + step, count)
        return at, (at // cols, lax.rem(at, cols))

    barrier = pltpu.get_barrier_semaphore()

    def greet(step, carry):
        pl.semaphore_signal(
            barrier, inc=1, device_id=peer(step)[1], device_id_type=pl.DeviceIdType.MESH
        )
        return carry

    lax.fori_loop(1, count, greet, 0)
    pl.semaphore_wait(barrier, count - 1)

    def scatter(step):
        at, device = peer(step)
        return pltpu.make_async_remote_copy(
            src_ref=x_ref.at[at], dst_ref=recv.at[step], send_sem=send_a.at[step],
            recv_sem=recv_a.at[step], device_id=device, device_id_type=pl.DeviceIdType.MESH,
        )

    def gather(step):
        device = peer(step)[1]
        return pltpu.make_async_remote_copy(
            src_ref=red, dst_ref=o_ref.at[me], send_sem=send_b.at[step],
            recv_sem=recv_b.at[step], device_id=device, device_id_type=pl.DeviceIdType.MESH,
        )

    def start(copy):
        def body(step, carry):
            copy(step).start()
            return carry
        lax.fori_loop(1, count, body, 0)

    start(scatter)

    def add(step, total):
        scatter(step).wait_recv()
        return total + recv[step]

    total = lax.fori_loop(1, count, add, x_ref[me])
    red[...] = total
    o_ref[me] = total
    start(gather)

    def finish(step, carry):
        gather(step).wait_recv()
        scatter(step).wait_send()
        gather(step).wait_send()
        return carry

    lax.fori_loop(1, count, finish, 0)


def sum_all(rows, cols, value, ident):
    count = rows * cols
    height, width = value.shape
    piece = height // count
    spec = pl.BlockSpec(memory_space=pltpu.VMEM)
    out = pl.pallas_call(
        functools.partial(sum_kernel, rows, cols),
        out_shape=jax.ShapeDtypeStruct((count, piece, width), jnp.float32),
        in_specs=[spec],
        out_specs=spec,
        scratch_shapes=[
            pltpu.VMEM((count, piece, width), jnp.float32),
            pltpu.VMEM((piece, width), jnp.float32),
            pltpu.SemaphoreType.DMA((count,)),
            pltpu.SemaphoreType.DMA((count,)),
            pltpu.SemaphoreType.DMA((count,)),
            pltpu.SemaphoreType.DMA((count,)),
        ],
        compiler_params=pltpu.CompilerParams(collective_id=ident, has_side_effects=True),
    )(value.reshape(count, piece, width))
    return out.reshape(height, width)


def shards(rows, cols, a_trail, a_panel, l_panel, a_diag, l_inverse):
    chips = cols // 2
    height = a_panel.shape[0]
    block_width = a_diag.shape[0]
    row_index = lax.axis_index("row")
    col_index = lax.axis_index("col")
    chip = col_index // 2
    core = col_index % 2
    me = row_index * cols + col_index
    sibling = [(c, c ^ 1) for c in range(cols)]

    def chip_shift(step):
        return [(c, (c + 2 * step) % cols) for c in range(cols)]

    def rows_from(shard):
        out = jnp.zeros((cols,) + shard.shape, jnp.float32)
        for step in range(chips):
            part = lax.ppermute(shard, "col", chip_shift(step)) if step else shard
            twin = lax.ppermute(part, "col", sibling)
            at = (col_index + cols - 2 * step) % cols
            out = lax.dynamic_update_index_in_dim(out, part, at, 0)
            out = lax.dynamic_update_index_in_dim(out, twin, at ^ 1, 0)
        return out.reshape(cols * shard.shape[0], shard.shape[1])

    def cols_from(shard):
        out = jnp.zeros((rows,) + shard.shape, jnp.float32)
        for step in range(rows):
            pairs = [
                (c * rows + (i + step) % rows, i * cols + c)
                for i in range(rows) for c in range(cols)
            ]
            part = lax.ppermute(shard, BOTH, pairs)
            out = lax.dynamic_update_index_in_dim(out, part, (row_index + step) % rows, 0)
        return out.reshape(rows * shard.shape[0], shard.shape[1])

    def sum_to_shard(values):
        parts = values.reshape(chips, 2, height, values.shape[1])

        def pick(to_chip, to_core):
            return lax.dynamic_slice(
                parts, (to_chip, to_core, 0, 0), (1, 1) + parts.shape[2:]
            ).reshape(parts.shape[2:])

        total = None
        for step in range(chips):
            to_chip = (chip + step) % chips
            both = pick(to_chip, core) + lax.ppermute(pick(to_chip, 1 - core), "col", sibling)
            if step:
                both = lax.ppermute(both, "col", chip_shift(step))
            total = both if total is None else total + both
        return total

    a_first = jnp.where(col_index == 0, a_trail[:height, :block_width], 0.0)
    for to in range(1, cols):
        a_first = a_first + lax.ppermute(
            a_trail[to * height : (to + 1) * height, :block_width], "col", [(0, to)]
        )
    a11_new = product(product(l_inverse, a_diag), l_inverse.T)
    solved = product(a_panel, l_inverse.T)
    half_term = 0.5 * product(l_panel, a11_new)
    first_y = solved - half_term
    panel_out = first_y - half_term
    pair = jnp.concatenate((first_y, l_panel), axis=1)
    tall = min(height, block_width)
    first_pair = sum_all(
        rows, cols,
        jnp.concatenate(
            [jnp.where(me == t, pair[:tall], 0.0) for t in range(block_width // tall)], axis=0
        ),
        0,
    )
    first_swap = jnp.concatenate(
        (first_pair[:, block_width:], first_pair[:, :block_width]), axis=1
    )
    panel = a_first - product(pair, first_swap.T)
    global_rows = me * height + lax.iota(jnp.int32, height)
    next_panel = jnp.where((global_rows >= block_width)[:, None], panel, 0.0)
    picker = (
        global_rows[:, None] - block_width == lax.iota(jnp.int32, block_width)[None, :]
    ).astype(jnp.float32)
    stats = sum_all(
        rows, cols,
        jnp.concatenate(
            (product(next_panel.T, next_panel), product(picker.T, next_panel)), axis=1
        ),
        1,
    )
    factor = jnp.linalg.cholesky(stats[:, :block_width])
    solved_rows = right_solve(
        factor, jnp.concatenate((next_panel, stats[:, block_width:]), axis=0)
    )
    identity = jnp.eye(block_width, dtype=jnp.float32)
    g_inverse = newton_inverse(identity + solved_rows[height:]).T
    refl = solved_rows[:height] + picker

    pair_rows = rows_from(pair)
    pair_cols = cols_from(pair)
    swap_cols = jnp.concatenate((pair_cols[:, block_width:], pair_cols[:, :block_width]), axis=1)
    updated = a_trail - large_product(pair_rows, swap_cols.T)

    refl_cols = cols_from(refl)
    x_shard = product(sum_to_shard(large_product(updated, refl_cols)), g_inverse)
    refl_rows = rows_from(refl)
    core_sum = sum_all(rows, cols, product(refl.T, x_shard), 2)
    half_core = 0.5 * product(g_inverse.T, core_sum)
    z_cols = cols_from(x_shard) - product(refl_cols, half_core)
    z_rows = rows_from(x_shard) - product(refl_rows, half_core)
    trail_out = updated - large_product(
        jnp.concatenate((z_rows, refl_rows), axis=1),
        jnp.concatenate((refl_cols, z_cols), axis=1).T,
    )
    return (trail_out, panel_out)


def solution(mesh):
    return jax.shard_map(
        functools.partial(shards, mesh.shape["row"], mesh.shape["col"]),
        mesh=mesh,
        in_specs=(P("row", "col"), P(BOTH, None), P(BOTH, None), P(), P()),
        out_specs=(P("row", "col"), P(BOTH, None)),
        check_vma=False,
    )
```

```python
import functools

import jax
import jax.numpy as jnp
from jax import lax
from jax.experimental import pallas as pl
from jax.experimental.layout import Layout, with_layout_constraint
from jax.experimental.pallas import tpu as pltpu
from jax.sharding import PartitionSpec as P

NS_STEPS = 8
BOTH = ("row", "col")


def product(left, right):
    return jnp.dot(left, right, precision=lax.Precision.HIGHEST, preferred_element_type=jnp.float32)


def large_product(left, right):
    return jnp.dot(left, right, precision=lax.Precision.HIGH, preferred_element_type=jnp.float32)


def newton_inverse(matrix):
    identity = jnp.eye(matrix.shape[0], dtype=jnp.float32)
    approx = identity
    for repeat in range(NS_STEPS):
        approx = product(approx, 2.0 * identity - product(matrix, approx))
    return approx


def right_solve(factor, values):
    return lax.linalg.triangular_solve(
        factor, values, left_side=False, lower=True, transpose_a=True
    )


def sum_kernel(rows, cols, x_ref, o_ref, recv, red, send_a, recv_a, send_b, recv_b):
    count = rows * cols
    me = lax.axis_index("row") * cols + lax.axis_index("col")

    def peer(step):
        at = lax.rem(me + step, count)
        return at, (at // cols, lax.rem(at, cols))

    barrier = pltpu.get_barrier_semaphore()

    def greet(step, carry):
        pl.semaphore_signal(
            barrier, inc=1, device_id=peer(step)[1], device_id_type=pl.DeviceIdType.MESH
        )
        return carry

    lax.fori_loop(1, count, greet, 0)
    pl.semaphore_wait(barrier, count - 1)

    def scatter(step):
        at, device = peer(step)
        return pltpu.make_async_remote_copy(
            src_ref=x_ref.at[at], dst_ref=recv.at[step], send_sem=send_a.at[step],
            recv_sem=recv_a.at[step], device_id=device, device_id_type=pl.DeviceIdType.MESH,
        )

    def gather(step):
        device = peer(step)[1]
        return pltpu.make_async_remote_copy(
            src_ref=red, dst_ref=o_ref.at[me], send_sem=send_b.at[step],
            recv_sem=recv_b.at[step], device_id=device, device_id_type=pl.DeviceIdType.MESH,
        )

    def start(copy):
        def body(step, carry):
            copy(step).start()
            return carry
        lax.fori_loop(1, count, body, 0)

    start(scatter)

    def add(step, total):
        scatter(step).wait_recv()
        return total + recv[step]

    total = lax.fori_loop(1, count, add, x_ref[me])
    red[...] = total
    o_ref[me] = total
    start(gather)

    def finish(step, carry):
        gather(step).wait_recv()
        scatter(step).wait_send()
        gather(step).wait_send()
        return carry

    lax.fori_loop(1, count, finish, 0)


def sum_all(rows, cols, value, ident):
    count = rows * cols
    height, width = value.shape
    piece = height // count
    spec = pl.BlockSpec(memory_space=pltpu.VMEM)
    out = pl.pallas_call(
        functools.partial(sum_kernel, rows, cols),
        out_shape=jax.ShapeDtypeStruct((count, piece, width), jnp.float32),
        in_specs=[spec],
        out_specs=spec,
        scratch_shapes=[
            pltpu.VMEM((count, piece, width), jnp.float32),
            pltpu.VMEM((piece, width), jnp.float32),
            pltpu.SemaphoreType.DMA((count,)),
            pltpu.SemaphoreType.DMA((count,)),
            pltpu.SemaphoreType.DMA((count,)),
            pltpu.SemaphoreType.DMA((count,)),
        ],
        compiler_params=pltpu.CompilerParams(collective_id=ident, has_side_effects=True),
    )(value.reshape(count, piece, width))
    return out.reshape(height, width)


def gather_kernel(rows, cols, x_ref, v_ref, x_rows, v_rows, x_cols, col_send, col_recv,
                  row_send, row_recv, twin_send, twin_recv, own_sem):
    chips = cols // 2
    i = lax.axis_index("row")
    c = lax.axis_index("col")
    me = i * cols + c
    core = lax.rem(c, 2)
    twin = c + 1 - 2 * core
    mesh_id = pl.DeviceIdType.MESH
    count = rows * cols
    barrier = pltpu.get_barrier_semaphore()

    def greet(step, carry):
        at = lax.rem(me + step, count)
        pl.semaphore_signal(
            barrier, inc=1, device_id=(at // cols, lax.rem(at, cols)), device_id_type=mesh_id
        )
        return carry

    lax.fori_loop(1, count, greet, 0)
    pl.semaphore_wait(barrier, count - 1)

    block = me // rows
    slot = lax.rem(me, rows)
    own = [
        pltpu.make_async_copy(x_ref, x_rows.at[c], own_sem.at[0]),
        pltpu.make_async_copy(v_ref, v_rows.at[c], own_sem.at[1]),
    ]
    own_col = pltpu.make_async_copy(x_ref, x_cols.at[slot], own_sem.at[2])

    def to_col(step):
        return pltpu.make_async_remote_copy(
            src_ref=x_ref, dst_ref=x_cols.at[slot], send_sem=col_send.at[step],
            recv_sem=col_recv.at[slot], device_id=(lax.rem(i + step, rows), block),
            device_id_type=mesh_id,
        )

    def from_col(k):
        return pltpu.make_async_remote_copy(
            src_ref=x_ref, dst_ref=x_cols.at[k], send_sem=col_send.at[0],
            recv_sem=col_recv.at[k], device_id=(i, twin), device_id_type=mesh_id,
        )

    pieces = ((x_ref, x_rows), (v_ref, v_rows))

    def to_row(which, step):
        src, dst = pieces[which]
        return pltpu.make_async_remote_copy(
            src_ref=src, dst_ref=dst.at[c], send_sem=row_send.at[which, step],
            recv_sem=row_recv.at[which, step],
            device_id=(i, lax.rem(c + 2 * step, cols)), device_id_type=mesh_id,
        )

    def to_twin(which, step):
        src, dst = pieces[which]
        at = lax.rem(c + cols - 2 * step, cols)
        return pltpu.make_async_remote_copy(
            src_ref=dst.at[at] if step else src, dst_ref=dst.at[at],
            send_sem=twin_send.at[which, step], recv_sem=twin_recv.at[which, step],
            device_id=(i, twin), device_id_type=mesh_id,
        )

    is_own = block == c
    for step in range(1, rows):
        to_col(step).start()

    @pl.when(is_own)
    def _():
        own_col.start()

    @pl.when(jnp.logical_not(is_own))
    def _():
        to_col(0).start()

    for which in range(2):
        for step in range(1, chips):
            to_row(which, step).start()
    for which in range(2):
        own[which].start()
        to_twin(which, 0).start()
    for which in range(2):
        for step in range(1, chips):
            to_row(which, step).wait_recv()
            to_twin(which, step).start()
    for which in range(2):
        for step in range(chips):
            to_twin(which, step).wait_recv()
    for k in range(rows):
        source_is_me = c * rows + k == me

        @pl.when(source_is_me)
        def _():
            own_col.wait()

        @pl.when(jnp.logical_not(source_is_me))
        def _(k=k):
            from_col(k).wait_recv()

    for which in range(2):
        own[which].wait()
        for step in range(chips):
            to_twin(which, step).wait_send()
            if step:
                to_row(which, step).wait_send()
    for step in range(1, rows):
        to_col(step).wait_send()

    @pl.when(jnp.logical_not(is_own))
    def _():
        to_col(0).wait_send()


def gather_both(rows, cols, x, v, ident):
    height, width = x.shape
    chips = cols // 2
    spec = pl.BlockSpec(memory_space=pl.ANY)
    tall = jax.ShapeDtypeStruct((cols, height, width), jnp.float32)
    x_rows, v_rows, x_cols = pl.pallas_call(
        functools.partial(gather_kernel, rows, cols),
        out_shape=(tall, tall, jax.ShapeDtypeStruct((rows, height, width), jnp.float32)),
        in_specs=[spec, spec],
        out_specs=(spec, spec, spec),
        scratch_shapes=[
            pltpu.SemaphoreType.DMA((rows,)),
            pltpu.SemaphoreType.DMA((rows,)),
            pltpu.SemaphoreType.DMA((2, chips)),
            pltpu.SemaphoreType.DMA((2, chips)),
            pltpu.SemaphoreType.DMA((2, chips)),
            pltpu.SemaphoreType.DMA((2, chips)),
            pltpu.SemaphoreType.DMA((3,)),
        ],
        compiler_params=pltpu.CompilerParams(collective_id=ident, has_side_effects=True),
    )(x, v)
    return (
        x_rows.reshape(-1, width), v_rows.reshape(-1, width), x_cols.reshape(-1, width)
    )


def shards(rows, cols, a_trail, a_panel, l_panel, a_diag, l_inverse):
    chips = cols // 2
    height = a_panel.shape[0]
    block_width = a_diag.shape[0]
    row_index = lax.axis_index("row")
    col_index = lax.axis_index("col")
    chip = col_index // 2
    core = col_index % 2
    me = row_index * cols + col_index
    sibling = [(c, c ^ 1) for c in range(cols)]

    def chip_shift(step):
        return [(c, (c + 2 * step) % cols) for c in range(cols)]

    def rows_from(shard):
        out = jnp.zeros((cols,) + shard.shape, jnp.float32)
        for step in range(chips):
            part = lax.ppermute(shard, "col", chip_shift(step)) if step else shard
            twin = lax.ppermute(part, "col", sibling)
            at = (col_index + cols - 2 * step) % cols
            out = lax.dynamic_update_index_in_dim(out, part, at, 0)
            out = lax.dynamic_update_index_in_dim(out, twin, at ^ 1, 0)
        return out.reshape(cols * shard.shape[0], shard.shape[1])

    def cols_from(shard):
        out = jnp.zeros((rows,) + shard.shape, jnp.float32)
        for step in range(rows):
            pairs = [
                (c * rows + (i + step) % rows, i * cols + c)
                for i in range(rows) for c in range(cols)
            ]
            part = lax.ppermute(shard, BOTH, pairs)
            out = lax.dynamic_update_index_in_dim(out, part, (row_index + step) % rows, 0)
        return out.reshape(rows * shard.shape[0], shard.shape[1])

    def sum_to_shard(values):
        parts = values.reshape(chips, 2, height, values.shape[1])

        def pick(to_chip, to_core):
            return lax.dynamic_slice(
                parts, (to_chip, to_core, 0, 0), (1, 1) + parts.shape[2:]
            ).reshape(parts.shape[2:])

        total = None
        for step in range(chips):
            to_chip = (chip + step) % chips
            both = pick(to_chip, core) + lax.ppermute(pick(to_chip, 1 - core), "col", sibling)
            if step:
                both = lax.ppermute(both, "col", chip_shift(step))
            total = both if total is None else total + both
        return total

    a_first = jnp.where(col_index == 0, a_trail[:height, :block_width], 0.0)
    for to in range(1, cols):
        a_first = a_first + lax.ppermute(
            a_trail[to * height : (to + 1) * height, :block_width], "col", [(0, to)]
        )
    a11_new = product(product(l_inverse, a_diag), l_inverse.T)
    solved = product(a_panel, l_inverse.T)
    half_term = 0.5 * product(l_panel, a11_new)
    first_y = solved - half_term
    panel_out = first_y - half_term
    pair = jnp.concatenate((first_y, l_panel), axis=1)
    tall = min(height, block_width)
    first_pair = sum_all(
        rows, cols,
        jnp.concatenate(
            [jnp.where(me == t, pair[:tall], 0.0) for t in range(block_width // tall)], axis=0
        ),
        0,
    )
    first_swap = jnp.concatenate(
        (first_pair[:, block_width:], first_pair[:, :block_width]), axis=1
    )
    panel = a_first - product(pair, first_swap.T)
    global_rows = me * height + lax.iota(jnp.int32, height)
    next_panel = jnp.where((global_rows >= block_width)[:, None], panel, 0.0)
    picker = (
        global_rows[:, None] - block_width == lax.iota(jnp.int32, block_width)[None, :]
    ).astype(jnp.float32)
    stats = sum_all(
        rows, cols,
        jnp.concatenate(
            (product(next_panel.T, next_panel), product(picker.T, next_panel)), axis=1
        ),
        1,
    )
    late_pair, stats = lax.optimization_barrier((pair, stats))
    late_pair = with_layout_constraint(late_pair, Layout(major_to_minor=(0, 1)))
    factor = jnp.linalg.cholesky(stats[:, :block_width])
    solved_rows = right_solve(
        factor, jnp.concatenate((next_panel, stats[:, block_width:]), axis=0)
    )
    identity = jnp.eye(block_width, dtype=jnp.float32)
    g_inverse = newton_inverse(identity + solved_rows[height:]).T
    refl = solved_rows[:height] + picker

    pair_rows = rows_from(late_pair)
    pair_cols = cols_from(late_pair)
    swap_cols = jnp.concatenate((pair_cols[:, block_width:], pair_cols[:, :block_width]), axis=1)
    updated = a_trail - large_product(pair_rows, swap_cols.T)

    refl_cols = cols_from(refl)
    x_shard = product(sum_to_shard(large_product(updated, refl_cols)), g_inverse)
    core_sum = sum_all(rows, cols, product(refl.T, x_shard), 2)
    half_core = 0.5 * product(g_inverse.T, core_sum)
    x_shard, refl, half_core = lax.optimization_barrier((x_shard, refl, half_core))
    x_rows, refl_rows, x_cols = gather_both(rows, cols, x_shard, refl, 3)
    z_cols = x_cols - product(refl_cols, half_core)
    z_rows = x_rows - product(refl_rows, half_core)
    trail_out = updated - large_product(
        jnp.concatenate((z_rows, refl_rows), axis=1),
        jnp.concatenate((refl_cols, z_cols), axis=1).T,
    )
    return (trail_out, panel_out)


def solution(mesh):
    return jax.shard_map(
        functools.partial(shards, mesh.shape["row"], mesh.shape["col"]),
        mesh=mesh,
        in_specs=(P("row", "col"), P(BOTH, None), P(BOTH, None), P(), P()),
        out_specs=(P("row", "col"), P(BOTH, None)),
        check_vma=False,
    )
```

```python
import functools

import jax
import jax.numpy as jnp
from jax import lax
from jax.experimental import pallas as pl
from jax.experimental.layout import Layout, with_layout_constraint
from jax.experimental.pallas import tpu as pltpu
from jax.sharding import PartitionSpec as P

NS_STEPS = 8
BOTH = ("row", "col")
MESH_ID = pl.DeviceIdType.MESH


def product(left, right):
    return jnp.dot(left, right, precision=lax.Precision.HIGHEST, preferred_element_type=jnp.float32)


def large_product(left, right):
    return jnp.dot(left, right, precision=lax.Precision.HIGH, preferred_element_type=jnp.float32)


def newton_inverse(matrix):
    identity = jnp.eye(matrix.shape[0], dtype=jnp.float32)
    approx = identity
    for _ in range(NS_STEPS):
        approx = product(approx, 2.0 * identity - product(matrix, approx))
    return approx


def right_solve(factor, values):
    return lax.linalg.triangular_solve(
        factor, values, left_side=False, lower=True, transpose_a=True
    )


def greet_all(rows, cols):
    count = rows * cols
    me = lax.axis_index("row") * cols + lax.axis_index("col")
    barrier = pltpu.get_barrier_semaphore()

    def greet(step, carry):
        at = lax.rem(me + step, count)
        pl.semaphore_signal(
            barrier, inc=1, device_id=(at // cols, lax.rem(at, cols)), device_id_type=MESH_ID
        )
        return carry

    lax.fori_loop(1, count, greet, 0)
    pl.semaphore_wait(barrier, count - 1)


def sum_steps(rows, cols, x_ref, o_ref, recv, red, send_a, recv_a, send_b, recv_b, held):
    count = rows * cols
    me = lax.axis_index("row") * cols + lax.axis_index("col")

    def peer(step):
        at = lax.rem(me + step, count)
        return at, (at // cols, lax.rem(at, cols))

    def owner(at):
        return (at * x_ref.shape[1]) // held

    def scatter(step):
        at, device = peer(step)
        return pltpu.make_async_remote_copy(
            src_ref=x_ref.at[at], dst_ref=recv.at[step], send_sem=send_a.at[step],
            recv_sem=recv_a.at[step], device_id=device, device_id_type=MESH_ID,
        )

    def gather(step):
        device = peer(step)[1]
        return pltpu.make_async_remote_copy(
            src_ref=red, dst_ref=o_ref.at[me], send_sem=send_b.at[step],
            recv_sem=recv_b.at[step], device_id=device, device_id_type=MESH_ID,
        )

    def loop(action):
        def body(step, carry):
            action(step)
            return carry

        lax.fori_loop(1, count, body, 0)

    def sends(step, action):
        if held is None:
            action()
        else:
            pl.when(owner(peer(step)[0]) == me)(action)

    def first():
        loop(lambda step: sends(step, lambda: scatter(step).start()))

    def second():
        if held is None:
            def add(step, total):
                scatter(step).wait_recv()
                return total + recv[step]

            total = lax.fori_loop(1, count, add, x_ref[me])
            red[...] = total
            o_ref[me] = total
        else:
            source = owner(me)

            @pl.when(source == me)
            def _():
                red[...] = x_ref[me]
                o_ref[me] = x_ref[me]

            @pl.when(source != me)
            def _():
                step = lax.rem(me + count - source, count)
                scatter(step).wait_recv()
                red[...] = recv[step]
                o_ref[me] = recv[step]
        loop(lambda step: gather(step).start())

    def third():
        def finish(step):
            gather(step).wait_recv()
            sends(step, lambda: scatter(step).wait_send())
            gather(step).wait_send()

        loop(finish)

    return first, second, third


def sum_scratch(count, piece, width):
    return [
        pltpu.VMEM((count, piece, width), jnp.float32),
        pltpu.VMEM((piece, width), jnp.float32),
        pltpu.SemaphoreType.DMA((count,)),
        pltpu.SemaphoreType.DMA((count,)),
        pltpu.SemaphoreType.DMA((count,)),
        pltpu.SemaphoreType.DMA((count,)),
    ]


def sum_kernel(rows, cols, *refs):
    first, second, third = sum_steps(rows, cols, *refs, None)
    greet_all(rows, cols)
    first()
    second()
    third()


def first_kernel(rows, cols, held, x_ref, a_ref, o_ref, a_first, recv, red, send_a, recv_a,
                 send_b, recv_b, send_p, recv_p, own_sem):
    i = lax.axis_index("row")
    c = lax.axis_index("col")
    height, width = a_first.shape
    first, second, third = sum_steps(
        rows, cols, x_ref, o_ref, recv, red, send_a, recv_a, send_b, recv_b, held
    )

    def piece(to):
        return pltpu.make_async_remote_copy(
            src_ref=a_ref.at[pl.ds(to * height, height), pl.ds(0, width)], dst_ref=a_first,
            send_sem=send_p.at[to], recv_sem=recv_p.at[0], device_id=(i, to),
            device_id_type=MESH_ID,
        )

    own = pltpu.make_async_copy(
        a_ref.at[pl.ds(0, height), pl.ds(0, width)], a_first, own_sem.at[0]
    )
    greet_all(rows, cols)
    first()

    @pl.when(c == 0)
    def _():
        own.start()
        for to in range(1, cols):
            piece(to).start()

    second()
    third()

    @pl.when(c == 0)
    def _():
        own.wait()
        for to in range(1, cols):
            piece(to).wait_send()

    @pl.when(c != 0)
    def _():
        piece(1).wait_recv()


def sum_all(rows, cols, value, ident):
    count = rows * cols
    height, width = value.shape
    piece = height // count
    spec = pl.BlockSpec(memory_space=pltpu.VMEM)
    out = pl.pallas_call(
        functools.partial(sum_kernel, rows, cols),
        out_shape=jax.ShapeDtypeStruct((count, piece, width), jnp.float32),
        in_specs=[spec],
        out_specs=spec,
        scratch_shapes=sum_scratch(count, piece, width),
        compiler_params=pltpu.CompilerParams(collective_id=ident, has_side_effects=True),
    )(value.reshape(count, piece, width))
    return out.reshape(height, width)


def first_exchange(rows, cols, value, held, a_trail, height, block_width, ident):
    count = rows * cols
    tall, width = value.shape
    piece = tall // count
    spec = pl.BlockSpec(memory_space=pltpu.VMEM)
    anywhere = pl.BlockSpec(memory_space=pl.ANY)
    out, a_first = pl.pallas_call(
        functools.partial(first_kernel, rows, cols, held),
        out_shape=(
            jax.ShapeDtypeStruct((count, piece, width), jnp.float32),
            jax.ShapeDtypeStruct((height, block_width), jnp.float32),
        ),
        in_specs=[spec, anywhere],
        out_specs=(spec, spec),
        scratch_shapes=sum_scratch(count, piece, width) + [
            pltpu.SemaphoreType.DMA((cols,)),
            pltpu.SemaphoreType.DMA((1,)),
            pltpu.SemaphoreType.DMA((1,)),
        ],
        compiler_params=pltpu.CompilerParams(collective_id=ident, has_side_effects=True),
    )(value.reshape(count, piece, width), a_trail)
    return out.reshape(tall, width), a_first


def gather_kernel(rows, cols, p_ref, x_ref, v_ref, o_ref, x_rows, v_rows, x_cols, recv, red,
                  send_a, recv_a, send_b, recv_b, col_send, col_recv, row_send, row_recv,
                  twin_send, twin_recv, own_sem):
    chips = cols // 2
    i = lax.axis_index("row")
    c = lax.axis_index("col")
    me = i * cols + c
    core = lax.rem(c, 2)
    twin = c + 1 - 2 * core
    first, second, third = sum_steps(
        rows, cols, p_ref, o_ref, recv, red, send_a, recv_a, send_b, recv_b, None
    )
    greet_all(rows, cols)
    first()

    block = me // rows
    slot = lax.rem(me, rows)
    own = [
        pltpu.make_async_copy(x_ref, x_rows.at[c], own_sem.at[0]),
        pltpu.make_async_copy(v_ref, v_rows.at[c], own_sem.at[1]),
    ]
    own_col = pltpu.make_async_copy(x_ref, x_cols.at[slot], own_sem.at[2])

    def to_col(step):
        return pltpu.make_async_remote_copy(
            src_ref=x_ref, dst_ref=x_cols.at[slot], send_sem=col_send.at[step],
            recv_sem=col_recv.at[slot], device_id=(lax.rem(i + step, rows), block),
            device_id_type=MESH_ID,
        )

    def from_col(k):
        return pltpu.make_async_remote_copy(
            src_ref=x_ref, dst_ref=x_cols.at[k], send_sem=col_send.at[0],
            recv_sem=col_recv.at[k], device_id=(i, twin), device_id_type=MESH_ID,
        )

    pieces = ((x_ref, x_rows), (v_ref, v_rows))

    def to_row(which, step):
        src, dst = pieces[which]
        return pltpu.make_async_remote_copy(
            src_ref=src, dst_ref=dst.at[c], send_sem=row_send.at[which, step],
            recv_sem=row_recv.at[which, step],
            device_id=(i, lax.rem(c + 2 * step, cols)), device_id_type=MESH_ID,
        )

    def to_twin(which, step):
        src, dst = pieces[which]
        at = lax.rem(c + cols - 2 * step, cols)
        return pltpu.make_async_remote_copy(
            src_ref=dst.at[at] if step else src, dst_ref=dst.at[at],
            send_sem=twin_send.at[which, step], recv_sem=twin_recv.at[which, step],
            device_id=(i, twin), device_id_type=MESH_ID,
        )

    is_own = block == c
    for step in range(1, rows):
        to_col(step).start()

    @pl.when(is_own)
    def _():
        own_col.start()

    @pl.when(jnp.logical_not(is_own))
    def _():
        to_col(0).start()

    for which in range(2):
        for step in range(1, chips):
            to_row(which, step).start()
    for which in range(2):
        own[which].start()
        to_twin(which, 0).start()
    second()
    for which in range(2):
        for step in range(1, chips):
            to_row(which, step).wait_recv()
            to_twin(which, step).start()
    for which in range(2):
        for step in range(chips):
            to_twin(which, step).wait_recv()
    for k in range(rows):
        source_is_me = c * rows + k == me

        @pl.when(source_is_me)
        def _():
            own_col.wait()

        @pl.when(jnp.logical_not(source_is_me))
        def _(k=k):
            from_col(k).wait_recv()

    for which in range(2):
        own[which].wait()
        for step in range(chips):
            to_twin(which, step).wait_send()
            if step:
                to_row(which, step).wait_send()
    third()
    for step in range(1, rows):
        to_col(step).wait_send()

    @pl.when(jnp.logical_not(is_own))
    def _():
        to_col(0).wait_send()


def gather_both(rows, cols, part, x, v, ident):
    height, width = x.shape
    chips = cols // 2
    count = rows * cols
    piece = width // count
    near = pl.BlockSpec(memory_space=pltpu.VMEM)
    spec = pl.BlockSpec(memory_space=pl.ANY)
    tall = jax.ShapeDtypeStruct((cols, height, width), jnp.float32)
    total, x_rows, v_rows, x_cols = pl.pallas_call(
        functools.partial(gather_kernel, rows, cols),
        out_shape=(
            jax.ShapeDtypeStruct((count, piece, width), jnp.float32), tall, tall,
            jax.ShapeDtypeStruct((rows, height, width), jnp.float32),
        ),
        in_specs=[near, spec, spec],
        out_specs=(near, spec, spec, spec),
        scratch_shapes=sum_scratch(count, piece, width) + [
            pltpu.SemaphoreType.DMA((rows,)),
            pltpu.SemaphoreType.DMA((rows,)),
            pltpu.SemaphoreType.DMA((2, chips)),
            pltpu.SemaphoreType.DMA((2, chips)),
            pltpu.SemaphoreType.DMA((2, chips)),
            pltpu.SemaphoreType.DMA((2, chips)),
            pltpu.SemaphoreType.DMA((3,)),
        ],
        compiler_params=pltpu.CompilerParams(collective_id=ident, has_side_effects=True),
    )(part.reshape(count, piece, width), x, v)
    return (
        total.reshape(width, width), x_rows.reshape(-1, width), v_rows.reshape(-1, width), x_cols.reshape(-1, width)
    )


def shards(rows, cols, a_trail, a_panel, l_panel, a_diag, l_inverse):
    chips = cols // 2
    height = a_panel.shape[0]
    block_width = a_diag.shape[0]
    row_index = lax.axis_index("row")
    col_index = lax.axis_index("col")
    chip = col_index // 2
    core = col_index % 2
    me = row_index * cols + col_index
    sibling = [(c, c ^ 1) for c in range(cols)]

    def chip_shift(step):
        return [(c, (c + 2 * step) % cols) for c in range(cols)]

    def rows_from(shard):
        out = jnp.zeros((cols,) + shard.shape, jnp.float32)
        for step in range(chips):
            part = lax.ppermute(shard, "col", chip_shift(step)) if step else shard
            twin = lax.ppermute(part, "col", sibling)
            at = (col_index + cols - 2 * step) % cols
            out = lax.dynamic_update_index_in_dim(out, part, at, 0)
            out = lax.dynamic_update_index_in_dim(out, twin, at ^ 1, 0)
        return out.reshape(cols * shard.shape[0], shard.shape[1])

    def cols_from(shard):
        out = jnp.zeros((rows,) + shard.shape, jnp.float32)
        for step in range(rows):
            pairs = [
                (c * rows + (i + step) % rows, i * cols + c)
                for i in range(rows) for c in range(cols)
            ]
            part = lax.ppermute(shard, BOTH, pairs)
            out = lax.dynamic_update_index_in_dim(out, part, (row_index + step) % rows, 0)
        return out.reshape(rows * shard.shape[0], shard.shape[1])

    def sum_to_shard(values):
        parts = values.reshape(chips, 2, height, values.shape[1])

        def pick(to_chip, to_core):
            return lax.dynamic_slice(
                parts, (to_chip, to_core, 0, 0), (1, 1) + parts.shape[2:]
            ).reshape(parts.shape[2:])

        total = None
        for step in range(chips):
            to_chip = (chip + step) % chips
            both = pick(to_chip, core) + lax.ppermute(pick(to_chip, 1 - core), "col", sibling)
            if step:
                both = lax.ppermute(both, "col", chip_shift(step))
            total = both if total is None else total + both
        return total

    a11_new = product(product(l_inverse, a_diag), l_inverse.T)
    solved = product(a_panel, l_inverse.T)
    half_term = 0.5 * product(l_panel, a11_new)
    first_y = solved - half_term
    panel_out = first_y - half_term
    pair = jnp.concatenate((first_y, l_panel), axis=1)
    tall = min(height, block_width)
    first_pair, a_first = first_exchange(
        rows, cols, jnp.concatenate([pair[:tall]] * (block_width // tall), axis=0), tall,
        a_trail, height, block_width, 0,
    )
    first_swap = jnp.concatenate(
        (first_pair[:, block_width:], first_pair[:, :block_width]), axis=1
    )
    panel = a_first - product(pair, first_swap.T)
    global_rows = me * height + lax.iota(jnp.int32, height)
    next_panel = jnp.where((global_rows >= block_width)[:, None], panel, 0.0)
    picker = (
        global_rows[:, None] - block_width == lax.iota(jnp.int32, block_width)[None, :]
    ).astype(jnp.float32)
    stats = sum_all(
        rows, cols,
        jnp.concatenate(
            (product(next_panel.T, next_panel), product(picker.T, next_panel)), axis=1
        ),
        1,
    )
    late_pair, stats = lax.optimization_barrier((pair, stats))
    late_pair = with_layout_constraint(late_pair, Layout(major_to_minor=(0, 1)))
    factor = jnp.linalg.cholesky(stats[:, :block_width])
    solved_rows = right_solve(
        factor, jnp.concatenate((next_panel, stats[:, block_width:]), axis=0)
    )
    identity = jnp.eye(block_width, dtype=jnp.float32)
    g_inverse = newton_inverse(identity + solved_rows[height:]).T
    refl = solved_rows[:height] + picker

    pair_rows = rows_from(late_pair)
    pair_cols = cols_from(late_pair)
    swap_cols = jnp.concatenate((pair_cols[:, block_width:], pair_cols[:, :block_width]), axis=1)
    updated = a_trail - large_product(pair_rows, swap_cols.T)

    refl_cols = cols_from(refl)
    x_shard = product(sum_to_shard(large_product(updated, refl_cols)), g_inverse)
    core_sum, x_rows, refl_rows, x_cols = gather_both(
        rows, cols, product(refl.T, x_shard), x_shard, refl, 3
    )
    half_core = 0.5 * product(g_inverse.T, core_sum)
    z_cols = x_cols - product(refl_cols, half_core)
    z_rows = x_rows - product(refl_rows, half_core)
    trail_out = updated - large_product(
        jnp.concatenate((z_rows, refl_rows), axis=1),
        jnp.concatenate((refl_cols, z_cols), axis=1).T,
    )
    return (trail_out, panel_out)


def layer(rows, cols, *args):
    return shards(rows, cols, *args)


def solution(mesh):
    rows, cols = mesh.shape["row"], mesh.shape["col"]
    return jax.shard_map(
        functools.partial(layer, rows, cols),
        mesh=mesh,
        in_specs=(P("row", "col"), P(BOTH, None), P(BOTH, None), P(), P()),
        out_specs=(P("row", "col"), P(BOTH, None)),
        check_vma=False,
    )
```

```python
import functools

import jax
import jax.numpy as jnp
from jax import lax
from jax.experimental import pallas as pl
from jax.experimental.layout import Layout, with_layout_constraint
from jax.experimental.pallas import tpu as pltpu
from jax.sharding import PartitionSpec as P

NS_STEPS = 8
BOTH = ("row", "col")
MESH_ID = pl.DeviceIdType.MESH


def product(left, right):
    return jnp.dot(left, right, precision=lax.Precision.HIGHEST, preferred_element_type=jnp.float32)


def large_product(left, right):
    return jnp.dot(left, right, precision=lax.Precision.HIGH, preferred_element_type=jnp.float32)


def newton_inverse(matrix):
    identity = jnp.eye(matrix.shape[0], dtype=jnp.float32)
    approx = identity
    for _ in range(NS_STEPS):
        approx = product(approx, 2.0 * identity - product(matrix, approx))
    return approx


def right_solve(factor, values):
    return lax.linalg.triangular_solve(
        factor, values, left_side=False, lower=True, transpose_a=True
    )


def greet_all(rows, cols):
    count = rows * cols
    me = lax.axis_index("row") * cols + lax.axis_index("col")
    barrier = pltpu.get_barrier_semaphore()

    def greet(step, carry):
        at = lax.rem(me + step, count)
        pl.semaphore_signal(
            barrier, inc=1, device_id=(at // cols, lax.rem(at, cols)), device_id_type=MESH_ID
        )
        return carry

    lax.fori_loop(1, count, greet, 0)
    pl.semaphore_wait(barrier, count - 1)


def sum_steps(rows, cols, x_ref, o_ref, recv, red, send_a, recv_a, send_b, recv_b, held):
    count = rows * cols
    me = lax.axis_index("row") * cols + lax.axis_index("col")

    def peer(step):
        at = lax.rem(me + step, count)
        return at, (at // cols, lax.rem(at, cols))

    def owner(at):
        return (at * x_ref.shape[1]) // held

    def scatter(step):
        at, device = peer(step)
        return pltpu.make_async_remote_copy(
            src_ref=x_ref.at[at], dst_ref=recv.at[step], send_sem=send_a.at[step],
            recv_sem=recv_a.at[step], device_id=device, device_id_type=MESH_ID,
        )

    def gather(step):
        device = peer(step)[1]
        return pltpu.make_async_remote_copy(
            src_ref=red, dst_ref=o_ref.at[me], send_sem=send_b.at[step],
            recv_sem=recv_b.at[step], device_id=device, device_id_type=MESH_ID,
        )

    def loop(action):
        def body(step, carry):
            action(step)
            return carry

        lax.fori_loop(1, count, body, 0)

    def sends(step, action):
        if held is None:
            action()
        else:
            pl.when(owner(peer(step)[0]) == me)(action)

    def first():
        loop(lambda step: sends(step, lambda: scatter(step).start()))

    def second():
        if held is None:
            def add(step, total):
                scatter(step).wait_recv()
                return total + recv[step]

            total = lax.fori_loop(1, count, add, x_ref[me])
            red[...] = total
            o_ref[me] = total
        else:
            source = owner(me)

            @pl.when(source == me)
            def _():
                red[...] = x_ref[me]
                o_ref[me] = x_ref[me]

            @pl.when(source != me)
            def _():
                step = lax.rem(me + count - source, count)
                scatter(step).wait_recv()
                red[...] = recv[step]
                o_ref[me] = recv[step]
        loop(lambda step: gather(step).start())

    def third():
        def finish(step):
            gather(step).wait_recv()
            sends(step, lambda: scatter(step).wait_send())
            gather(step).wait_send()

        loop(finish)

    return first, second, third


def sum_scratch(count, piece, width):
    return [
        pltpu.VMEM((count, piece, width), jnp.float32),
        pltpu.VMEM((piece, width), jnp.float32),
        pltpu.SemaphoreType.DMA((count,)),
        pltpu.SemaphoreType.DMA((count,)),
        pltpu.SemaphoreType.DMA((count,)),
        pltpu.SemaphoreType.DMA((count,)),
    ]


def sum_kernel(rows, cols, *refs):
    first, second, third = sum_steps(rows, cols, *refs, None)
    greet_all(rows, cols)
    first()
    second()
    third()


def first_kernel(rows, cols, held, x_ref, a_ref, o_ref, a_first, recv, red, send_a, recv_a,
                 send_b, recv_b, send_p, recv_p, own_sem):
    i = lax.axis_index("row")
    c = lax.axis_index("col")
    height, width = a_first.shape
    first, second, third = sum_steps(
        rows, cols, x_ref, o_ref, recv, red, send_a, recv_a, send_b, recv_b, held
    )

    def piece(to):
        return pltpu.make_async_remote_copy(
            src_ref=a_ref.at[pl.ds(to * height, height), pl.ds(0, width)], dst_ref=a_first,
            send_sem=send_p.at[to], recv_sem=recv_p.at[0], device_id=(i, to),
            device_id_type=MESH_ID,
        )

    own = pltpu.make_async_copy(
        a_ref.at[pl.ds(0, height), pl.ds(0, width)], a_first, own_sem.at[0]
    )
    greet_all(rows, cols)
    first()

    @pl.when(c == 0)
    def _():
        own.start()
        for to in range(1, cols):
            piece(to).start()

    second()
    third()

    @pl.when(c == 0)
    def _():
        own.wait()
        for to in range(1, cols):
            piece(to).wait_send()

    @pl.when(c != 0)
    def _():
        piece(1).wait_recv()


def sum_all(rows, cols, value, ident):
    count = rows * cols
    height, width = value.shape
    piece = height // count
    spec = pl.BlockSpec(memory_space=pltpu.VMEM)
    out = pl.pallas_call(
        functools.partial(sum_kernel, rows, cols),
        out_shape=jax.ShapeDtypeStruct((count, piece, width), jnp.float32),
        in_specs=[spec],
        out_specs=spec,
        scratch_shapes=sum_scratch(count, piece, width),
        compiler_params=pltpu.CompilerParams(collective_id=ident, has_side_effects=True),
    )(value.reshape(count, piece, width))
    return out.reshape(height, width)


def first_exchange(rows, cols, value, held, a_trail, height, block_width, ident):
    count = rows * cols
    tall, width = value.shape
    piece = tall // count
    spec = pl.BlockSpec(memory_space=pltpu.VMEM)
    anywhere = pl.BlockSpec(memory_space=pl.ANY)
    out, a_first = pl.pallas_call(
        functools.partial(first_kernel, rows, cols, held),
        out_shape=(
            jax.ShapeDtypeStruct((count, piece, width), jnp.float32),
            jax.ShapeDtypeStruct((height, block_width), jnp.float32),
        ),
        in_specs=[spec, anywhere],
        out_specs=(spec, spec),
        scratch_shapes=sum_scratch(count, piece, width) + [
            pltpu.SemaphoreType.DMA((cols,)),
            pltpu.SemaphoreType.DMA((1,)),
            pltpu.SemaphoreType.DMA((1,)),
        ],
        compiler_params=pltpu.CompilerParams(collective_id=ident, has_side_effects=True),
    )(value.reshape(count, piece, width), a_trail)
    return out.reshape(tall, width), a_first


def gather_kernel(rows, cols, p_ref, x_ref, v_ref, o_ref, x_rows, v_rows, x_cols, recv, red,
                  send_a, recv_a, send_b, recv_b, col_send, col_recv, row_send, row_recv,
                  twin_send, twin_recv, own_sem):
    chips = cols // 2
    i = lax.axis_index("row")
    c = lax.axis_index("col")
    me = i * cols + c
    core = lax.rem(c, 2)
    twin = c + 1 - 2 * core
    first, second, third = sum_steps(
        rows, cols, p_ref, o_ref, recv, red, send_a, recv_a, send_b, recv_b, None
    )
    greet_all(rows, cols)
    first()

    block = me // rows
    slot = lax.rem(me, rows)
    own = [
        pltpu.make_async_copy(x_ref, x_rows.at[c], own_sem.at[0]),
        pltpu.make_async_copy(v_ref, v_rows.at[c], own_sem.at[1]),
    ]
    own_col = pltpu.make_async_copy(x_ref, x_cols.at[slot], own_sem.at[2])

    def to_col(step):
        return pltpu.make_async_remote_copy(
            src_ref=x_ref, dst_ref=x_cols.at[slot], send_sem=col_send.at[step],
            recv_sem=col_recv.at[slot], device_id=(lax.rem(i + step, rows), block),
            device_id_type=MESH_ID,
        )

    def from_col(k):
        return pltpu.make_async_remote_copy(
            src_ref=x_ref, dst_ref=x_cols.at[k], send_sem=col_send.at[0],
            recv_sem=col_recv.at[k], device_id=(i, twin), device_id_type=MESH_ID,
        )

    pieces = ((x_ref, x_rows), (v_ref, v_rows))

    def to_row(which, step):
        src, dst = pieces[which]
        return pltpu.make_async_remote_copy(
            src_ref=src, dst_ref=dst.at[c], send_sem=row_send.at[which, step],
            recv_sem=row_recv.at[which, step],
            device_id=(i, lax.rem(c + 2 * step, cols)), device_id_type=MESH_ID,
        )

    def to_twin(which, step):
        src, dst = pieces[which]
        at = lax.rem(c + cols - 2 * step, cols)
        return pltpu.make_async_remote_copy(
            src_ref=dst.at[at] if step else src, dst_ref=dst.at[at],
            send_sem=twin_send.at[which, step], recv_sem=twin_recv.at[which, step],
            device_id=(i, twin), device_id_type=MESH_ID,
        )

    is_own = block == c
    for step in range(1, rows):
        to_col(step).start()

    @pl.when(is_own)
    def _():
        own_col.start()

    @pl.when(jnp.logical_not(is_own))
    def _():
        to_col(0).start()

    for which in range(2):
        for step in range(1, chips):
            to_row(which, step).start()
    for which in range(2):
        own[which].start()
        to_twin(which, 0).start()
    second()
    for which in range(2):
        for step in range(1, chips):
            to_row(which, step).wait_recv()
            to_twin(which, step).start()
    for which in range(2):
        for step in range(chips):
            to_twin(which, step).wait_recv()
    for k in range(rows):
        source_is_me = c * rows + k == me

        @pl.when(source_is_me)
        def _():
            own_col.wait()

        @pl.when(jnp.logical_not(source_is_me))
        def _(k=k):
            from_col(k).wait_recv()

    for which in range(2):
        own[which].wait()
        for step in range(chips):
            to_twin(which, step).wait_send()
            if step:
                to_row(which, step).wait_send()
    third()
    for step in range(1, rows):
        to_col(step).wait_send()

    @pl.when(jnp.logical_not(is_own))
    def _():
        to_col(0).wait_send()


def gather_both(rows, cols, part, x, v, ident):
    height, width = x.shape
    chips = cols // 2
    count = rows * cols
    piece = width // count
    near = pl.BlockSpec(memory_space=pltpu.VMEM)
    spec = pl.BlockSpec(memory_space=pl.ANY)
    tall = jax.ShapeDtypeStruct((cols, height, width), jnp.float32)
    total, x_rows, v_rows, x_cols = pl.pallas_call(
        functools.partial(gather_kernel, rows, cols),
        out_shape=(
            jax.ShapeDtypeStruct((count, piece, width), jnp.float32), tall, tall,
            jax.ShapeDtypeStruct((rows, height, width), jnp.float32),
        ),
        in_specs=[near, spec, spec],
        out_specs=(near, spec, spec, spec),
        scratch_shapes=sum_scratch(count, piece, width) + [
            pltpu.SemaphoreType.DMA((rows,)),
            pltpu.SemaphoreType.DMA((rows,)),
            pltpu.SemaphoreType.DMA((2, chips)),
            pltpu.SemaphoreType.DMA((2, chips)),
            pltpu.SemaphoreType.DMA((2, chips)),
            pltpu.SemaphoreType.DMA((2, chips)),
            pltpu.SemaphoreType.DMA((3,)),
        ],
        compiler_params=pltpu.CompilerParams(collective_id=ident, has_side_effects=True),
    )(part.reshape(count, piece, width), x, v)
    return (
        total.reshape(width, width), x_rows.reshape(-1, width), v_rows.reshape(-1, width), x_cols.reshape(-1, width)
    )


def shards(rows, cols, a_trail, a_panel, l_panel, a_diag, l_inverse):
    chips = cols // 2
    height = a_panel.shape[0]
    block_width = a_diag.shape[0]
    row_index = lax.axis_index("row")
    col_index = lax.axis_index("col")
    chip = col_index // 2
    core = col_index % 2
    me = row_index * cols + col_index
    sibling = [(c, c ^ 1) for c in range(cols)]

    def chip_shift(step):
        return [(c, (c + 2 * step) % cols) for c in range(cols)]

    def rows_from(shard):
        out = jnp.zeros((cols,) + shard.shape, jnp.float32)
        for step in range(chips):
            part = lax.ppermute(shard, "col", chip_shift(step)) if step else shard
            twin = lax.ppermute(part, "col", sibling)
            at = (col_index + cols - 2 * step) % cols
            out = lax.dynamic_update_index_in_dim(out, part, at, 0)
            out = lax.dynamic_update_index_in_dim(out, twin, at ^ 1, 0)
        return out.reshape(cols * shard.shape[0], shard.shape[1])

    def cols_from(shard):
        out = jnp.zeros((rows,) + shard.shape, jnp.float32)
        for step in range(rows):
            pairs = [
                (c * rows + (i + step) % rows, i * cols + c)
                for i in range(rows) for c in range(cols)
            ]
            part = lax.ppermute(shard, BOTH, pairs)
            out = lax.dynamic_update_index_in_dim(out, part, (row_index + step) % rows, 0)
        return out.reshape(rows * shard.shape[0], shard.shape[1])

    def sum_to_shard(values):
        parts = values.reshape(chips, 2, height, values.shape[1])

        def pick(to_chip, to_core):
            return lax.dynamic_slice(
                parts, (to_chip, to_core, 0, 0), (1, 1) + parts.shape[2:]
            ).reshape(parts.shape[2:])

        total = None
        for step in range(chips):
            to_chip = (chip + step) % chips
            both = pick(to_chip, core) + lax.ppermute(pick(to_chip, 1 - core), "col", sibling)
            if step:
                both = lax.ppermute(both, "col", chip_shift(step))
            total = both if total is None else total + both
        return total

    a11_new = product(product(l_inverse, a_diag), l_inverse.T)
    solved = product(a_panel, l_inverse.T)
    half_term = 0.5 * product(l_panel, a11_new)
    first_y = solved - half_term
    panel_out = first_y - half_term
    pair = jnp.concatenate((first_y, l_panel), axis=1)
    tall = min(height, block_width)
    first_pair, a_first = first_exchange(
        rows, cols, jnp.concatenate([pair[:tall]] * (block_width // tall), axis=0), tall,
        a_trail, height, block_width, 0,
    )
    first_swap = jnp.concatenate(
        (first_pair[:, block_width:], first_pair[:, :block_width]), axis=1
    )
    panel = a_first - product(pair, first_swap.T)
    global_rows = me * height + lax.iota(jnp.int32, height)
    next_panel = jnp.where((global_rows >= block_width)[:, None], panel, 0.0)
    picker = (
        global_rows[:, None] - block_width == lax.iota(jnp.int32, block_width)[None, :]
    ).astype(jnp.float32)
    stats = sum_all(
        rows, cols,
        jnp.concatenate(
            (product(next_panel.T, next_panel), product(picker.T, next_panel)), axis=1
        ),
        1,
    )
    late_pair, stats = lax.optimization_barrier((pair, stats))
    late_pair = with_layout_constraint(late_pair, Layout(major_to_minor=(0, 1)))
    factor = jnp.linalg.cholesky(stats[:, :block_width])
    solved_rows = right_solve(
        factor, jnp.concatenate((next_panel, stats[:, block_width:]), axis=0)
    )
    identity = jnp.eye(block_width, dtype=jnp.float32)
    g_inverse = newton_inverse(identity + solved_rows[height:]).T
    refl = solved_rows[:height] + picker

    pair_rows = rows_from(late_pair)
    pair_cols = cols_from(late_pair)
    swap_cols = jnp.concatenate((pair_cols[:, block_width:], pair_cols[:, :block_width]), axis=1)
    updated = a_trail - large_product(pair_rows, swap_cols.T)

    refl_cols = cols_from(refl)
    x_shard = product(sum_to_shard(large_product(updated, refl_cols)), g_inverse)
    core_sum, x_rows, refl_rows, x_cols = gather_both(
        rows, cols, product(refl.T, x_shard), x_shard, refl, 3
    )
    half_core = 0.5 * product(g_inverse.T, core_sum)
    z_cols = x_cols - product(refl_cols, half_core + half_core.T)
    trail_out = updated - large_product(
        jnp.concatenate((x_rows, refl_rows), axis=1),
        jnp.concatenate((refl_cols, z_cols), axis=1).T,
    )
    return (trail_out, panel_out)


def layer(rows, cols, *args):
    return shards(rows, cols, *args)


def solution(mesh):
    rows, cols = mesh.shape["row"], mesh.shape["col"]
    return jax.shard_map(
        functools.partial(layer, rows, cols),
        mesh=mesh,
        in_specs=(P("row", "col"), P(BOTH, None), P(BOTH, None), P(), P()),
        out_specs=(P("row", "col"), P(BOTH, None)),
        check_vma=False,
    )
```
